32 devices in a mesh: blk: 16 (over z, y, core), rep: 2 (over x).
Axes of the slice: x: 2, y: 2, z: 4, core: 2. Of those that a mesh axis runs over, the one named last changes fastest.
Arguments:
- examples: float32 [8192, 1024], P(('blk', 'rep')), may hold values from -6 to 6
- targets: float32 [8192, 1000], P(('blk', 'rep')), may hold values from -6 to 6
- hop_reach: int32 [8192], P(('blk', 'rep')), may hold values from 1 to 5
- centers: float32 [4096, 1024], P('blk'), may hold values from -6 to 6
- coeffs: float32 [4096, 1000], P('blk'), may hold values from -0.15625 to 0.15625
- step_gain: float32 [4096], P('blk'), may hold values from 0.5 to 2
Outputs:
- new_coeffs: float32 [4096, 1000], P('blk')
- residual: float32 [8192, 1000], P(('blk', 'rep'))
The draws below stay inside these ranges and needn't reach their ends.
All inputs are finite; a program needn't handle non-finite values.
Results may differ from the reference program's by a relative error of at most 0.0003.
Values sent between devices are 32-bit elements; how exact they have to be, the bound alone decides.
No kernel may reach another device: no remote copies, remote signals or barrier semaphores. Data moves between devices by JAX's collectives and lax.ppermute only.
A program may use at most 64 MiB of HBM per device.

```python
import math
import jax
import jax.numpy as jnp
from jax import lax

D = 1024
OUT = 1000
CB = 256
HOPS = 4
EX_DEV = 256
EXAMPLES = 8192
CENTERS = 4096
N_BLK = 16
N_REP = 2


def place_ends(drawn, rng, low, high):
    place = [jax.random.randint(jax.random.fold_in(rng, axis), (), 0, length) for axis, length in enumerate(drawn.shape)]
    longest = drawn.shape.index(max(drawn.shape))
    neighbour = place[:longest] + [(place[longest] + 1) % drawn.shape[longest]] + place[longest + 1:]
    return drawn.at[tuple(place)].set(low).at[tuple(neighbour)].set(high)


def block_levels(stream_key, shape, shards, least, high):
    loudness, own = 1.0, jax.random.fold_in(stream_key, 6)
    for position, parts in shards:
        steps = jnp.exp(jax.random.uniform(jax.random.fold_in(own, position), (parts,), jnp.float32, least / len(shards), high / len(shards)))
        loudness = loudness * jnp.repeat(steps, shape[position] // parts).reshape([-1 if axis == position else 1 for axis in range(len(shape))])
    return loudness


def gaussian(key, dims, deviation, limit, cuts=(), dtype=jnp.bfloat16):
    entries = jax.random.normal(key, dims, jnp.float32) * deviation
    if len(cuts) > 0:
        entries = block_levels(key, dims, cuts, -0.22, 0.18) * entries
    return jnp.clip(entries, min=-limit, max=limit).astype(dtype)


def setup_inputs(seed: int = 0) -> dict:
    key_list = jax.random.split(jax.random.key(seed), 7)
    return {
        "examples": gaussian(key_list[0], (EXAMPLES, D), 1.0, 6.0, ((0, 32),), jnp.float32),
        "targets": gaussian(key_list[1], (EXAMPLES, OUT), 1.0, 6.0, ((0, 32),), jnp.float32),
        "hop_reach": place_ends(jax.random.randint(key_list[2], (EXAMPLES,), 1, HOPS + 2), jax.random.fold_in(key_list[2], 1), 1, (HOPS + 2) - 1).astype(jnp.int32),
        "centers": gaussian(key_list[3], (CENTERS, D), 1.0, 6.0, ((0, 16),), jnp.float32),
        "coeffs": gaussian(key_list[4], (CENTERS, OUT), (CB * (HOPS + 1)) ** -0.5, 0.15625, ((0, 16),), jnp.float32),
        "step_gain": jnp.clip(jnp.exp(math.log(2.0) - 1.3862944 * jax.random.uniform(key_list[5], (CENTERS,), jnp.float32) ** block_levels(key_list[5], (CENTERS,), ((0, 16),), -0.2, 0.2)), 0.5, 2.0),
    }


def reference(examples, targets, hop_reach, centers, coeffs, step_gain):
    rows = N_REP * EX_DEV
    grouped = examples.reshape(N_BLK, rows, D)
    wanted = targets.reshape(N_BLK, rows, OUT)
    reaches = hop_reach.reshape(N_BLK, rows)
    center_blocks = centers.reshape(N_BLK, CB, D)
    coeff_blocks = coeffs.reshape(N_BLK, CB, OUT)
    sharpness = 0.5 / math.sqrt(D)
    kernels = []
    predicted = jnp.zeros((N_BLK, rows, OUT), jnp.float32)
    for distance in range(HOPS + 1):
        seen_centers = jnp.roll(center_blocks, distance, axis=0)
        seen_coeffs = jnp.roll(coeff_blocks, distance, axis=0)
        scores = jnp.einsum('brd,bcd->brc', grouped, seen_centers, precision=lax.Precision.HIGHEST)
        visible = (reaches > distance).astype(jnp.float32)[:, :, None]
        kernel = jnp.exp(sharpness * scores) * visible
        kernels.append(kernel)
        predicted = predicted + jnp.einsum('brc,bco->bro', kernel, seen_coeffs, precision=lax.Precision.HIGHEST)
    residual = predicted - wanted
    gradient = jnp.zeros((N_BLK, CB, OUT), jnp.float32)
    for distance in range(HOPS + 1):
        term = jnp.einsum('brc,bro->bco', kernels[distance], residual, precision=lax.Precision.HIGHEST)
        gradient = gradient + jnp.roll(term, -distance, axis=0)
    step_size = 1.0 / math.sqrt(EX_DEV * N_REP * (HOPS + 1))
    new_coeffs = coeffs - (step_size * step_gain)[:, None] * gradient.reshape(CENTERS, OUT)
    return (new_coeffs, residual.reshape(EXAMPLES, OUT))
```

```python
import math

import jax
import jax.numpy as jnp
from jax import lax
from jax.sharding import PartitionSpec as P

HOPS = 4
CORES = 2
LANES = 128
FEATURE_PIECES = 4
COLUMN_PIECES = 2
PRECISION = lax.Precision.HIGH


def shifted(block, axis, distance):
    n = lax.axis_size(axis)
    return lax.ppermute(block, axis, [((i - distance) % n, i) for i in range(n)])


def swapped(block, bit):
    n = lax.axis_size("blk")
    return lax.ppermute(block, "blk", [(i, i ^ bit) for i in range(n)])


def product(a, b, da, db):
    return lax.dot_general(
        a,
        b,
        (((da,), (db,)), ((), ())),
        precision=PRECISION,
        preferred_element_type=jnp.float32,
    )


def total(terms):
    out = terms[0]
    for term in terms[1:]:
        out = out + term
    return out


def on_device(examples, targets, hop_reach, centers, coeffs, step_gain):
    rows, features = examples.shape
    outputs = targets.shape[1]
    n_rep = lax.axis_size("rep")
    rep = lax.axis_index("rep")
    blk = lax.axis_index("blk")
    core = blk % CORES
    odd = (blk // CORES) % 2 == 1
    far = 2 * CORES
    sharpness = 0.5 / math.sqrt(features)
    half = -(-outputs // (n_rep * LANES)) * LANES
    fill = ((0, 0), (0, n_rep * half - outputs))
    wide = half // COLUMN_PIECES
    deep = features // FEATURE_PIECES

    def columns(block, position):
        start = (position % n_rep) * half
        return lax.dynamic_slice(jnp.pad(block, fill), (0, start), (block.shape[0], half))

    def widths(block):
        return [block[:, i * wide : (i + 1) * wide] for i in range(COLUMN_PIECES)]

    def depths(block):
        return [block[:, i * deep : (i + 1) * deep] for i in range(FEATURE_PIECES)]

    near0 = depths(centers)
    coeff_half = columns(coeffs, rep)
    w0 = widths(coeff_half)
    far_c = [shifted(p, "blk", far) for p in near0]
    far_w = [shifted(p, "blk", far) for p in w0]
    mid_c = [swapped(jnp.where(odd, a, p), CORES) for a, p in zip(far_c, near0)]
    mid_w = [swapped(jnp.where(odd, a, p), CORES) for a, p in zip(far_w, w0)]

    own_rows = [examples] + [shifted(examples, "rep", s) for s in range(1, n_rep)]
    other_rows = [swapped(e, 1) for e in own_rows]
    own_reach = jnp.concatenate(
        [hop_reach] + [shifted(hop_reach, "rep", s) for s in range(1, n_rep)]
    )
    other_reach = swapped(own_reach, 1)
    own_target = jnp.concatenate(
        [columns(targets, rep)]
        + [shifted(columns(targets, rep + s), "rep", s) for s in range(1, n_rep)]
    )
    other_target = swapped(own_target, 1)

    def kernel_of(row_sets, reach, hop, pieces):
        scores = []
        for e in row_sets:
            if pieces is None:
                scores.append(product(e, centers, 1, 1))
            else:
                scores.append(
                    total([product(x, c, 1, 1) for x, c in zip(depths(e), pieces)])
                )
        visible = ((reach > hop) & (hop >= 0)).astype(jnp.float32)[:, None]
        return jnp.exp(sharpness * jnp.concatenate(scores)) * visible

    blocks = (None, mid_c, far_c)
    own_k, other_k = [], []
    for j, pieces in enumerate(blocks):
        own_k.append(kernel_of(own_rows, own_reach, CORES * j, pieces))
        other_k.append(
            kernel_of(other_rows, other_reach, CORES * j + 1 - 2 * core, pieces)
        )

    step_size = 1.0 / math.sqrt(rows * n_rep * (HOPS + 1))
    factor = (step_size * step_gain)[:, None]
    order = (0, 2, 1)
    residuals = [[] for _ in range(n_rep)]
    updated = [[] for _ in range(n_rep)]
    for i in range(COLUMN_PIECES):
        w = (w0[i], mid_w[i], far_w[i])
        own_p = total([product(own_k[j], w[j], 1, 0) for j in order])
        other_p = total([product(other_k[j], w[j], 1, 0) for j in order])
        cut = slice(i * wide, (i + 1) * wide)
        own_r = own_p + swapped(other_p, 1) - own_target[:, cut]
        other_r = other_p + swapped(own_p, 1) - other_target[:, cut]
        grad = [
            product(own_k[j], own_r, 0, 0) + product(other_k[j], other_r, 0, 0)
            for j in range(3)
        ]
        across = swapped(grad[1], CORES)
        back = shifted(grad[2] + jnp.where(odd, across, 0.0), "blk", -far)
        gradient = grad[0] + jnp.where(odd, 0.0, across) + back
        new = w0[i] - factor * gradient
        for s in range(n_rep):
            mine = own_r[s * rows : (s + 1) * rows]
            residuals[s].append(shifted(mine, "rep", -s) if s else mine)
            updated[s].append(shifted(new, "rep", -s) if s else new)

    def assembled(received):
        parts = [jnp.concatenate(p, axis=1) for p in received]
        placed = []
        for q in range(n_rep):
            part = parts[0]
            for s in range(1, n_rep):
                part = jnp.where((rep + s) % n_rep == q, parts[s], part)
            placed.append(part)
        return jnp.concatenate(placed, axis=1)[:, :outputs]

    return (assembled(updated), assembled(residuals))


def solution(mesh):
    in_specs = (
        P(("blk", "rep"), None),
        P(("blk", "rep"), None),
        P(("blk", "rep")),
        P("blk", None),
        P("blk", None),
        P("blk"),
    )
    out_specs = (P("blk", None), P(("blk", "rep"), None))
    return jax.shard_map(
        on_device, mesh=mesh, in_specs=in_specs, out_specs=out_specs, check_vma=False
    )
```

```python
import math

import jax
import jax.numpy as jnp
from jax import lax
from jax.experimental import pallas as pl
from jax.experimental.pallas import tpu as pltpu
from jax.sharding import PartitionSpec as P


HOPS = 4
CORES = 2
LANES = 128
PIECES = 4
CHUNKS = 2
PRECISION = lax.Precision.HIGH
ANY = pl.BlockSpec(memory_space=pl.ANY)
F32 = jnp.float32


def shifted(block, axis, distance):
    n = lax.axis_size(axis)
    return lax.ppermute(block, axis, [((i - distance) % n, i) for i in range(n)])


def swapped(block, bit):
    n = lax.axis_size("blk")
    return lax.ppermute(block, "blk", [(i, i ^ bit) for i in range(n)])


def product(a, b, da, db):
    return lax.dot_general(
        a, b, (((da,), (db,)), ((), ())), precision=PRECISION, preferred_element_type=F32
    )


def shape(*dims):
    return jax.ShapeDtypeStruct(dims, F32)


def split(block):
    rows, width = block.shape
    deep = width // PIECES

    def body(src, *refs):
        sems = refs[-1]
        copies = [
            pltpu.make_async_copy(
                src.at[:, pl.ds(i * deep, deep)], refs[i], sems.at[i]
            )
            for i in range(PIECES)
        ]
        for c in copies:
            c.start()
        for c in copies:
            c.wait()

    return pl.pallas_call(
        body,
        out_shape=[shape(rows, deep)] * PIECES,
        in_specs=[ANY],
        out_specs=[ANY] * PIECES,
        scratch_shapes=[pltpu.SemaphoreType.DMA((PIECES,))],
    )(block)


def halves(coeffs, targets, n_rep, half):
    wide = half // CHUNKS

    def body(w, t, *outs):
        rep = lax.axis_index("rep")
        rows, outputs = w.shape

        def columns(src, q, start, size):
            low, high = q * half + start, min(q * half + start + size, outputs)
            value = src[:, low:high]
            if high - low < size:
                rest = jnp.zeros((rows, low + size - high), F32)
                value = jnp.concatenate([value, rest], axis=1)
            return value

        for q in range(n_rep):

            @pl.when(rep == q)
            def _():
                for i in range(CHUNKS):
                    outs[i][...] = columns(w, q, i * wide, wide)
                for s in range(n_rep):
                    outs[CHUNKS + s][...] = columns(t, (q + s) % n_rep, 0, half)

    rows = coeffs.shape[0]
    return pl.pallas_call(
        body,
        out_shape=[shape(rows, wide)] * CHUNKS + [shape(rows, half)] * n_rep,
    )(coeffs, targets)


def relay(own, received):
    def body(own_ref, received_ref, out, sem):
        odd = (lax.axis_index("blk") // CORES) % 2 == 1

        @pl.when(odd)
        def _():
            copy = pltpu.make_async_copy(received_ref, out, sem)
            copy.start()
            copy.wait()

        @pl.when(jnp.logical_not(odd))
        def _():
            copy = pltpu.make_async_copy(own_ref, out, sem)
            copy.start()
            copy.wait()

    return pl.pallas_call(
        body,
        out_shape=shape(*own.shape),
        in_specs=[ANY, ANY],
        out_specs=ANY,
        scratch_shapes=[pltpu.SemaphoreType.DMA],
    )(own, received)


def kernel_block(row_sets, center_pieces, reach, hop, sharpness):
    n_sets = len(row_sets)
    rows, features = row_sets[0].shape
    n_centers = center_pieces[0].shape[0]
    deep = features // PIECES

    def body(*refs):
        sets, refs = refs[:n_sets], refs[n_sets:]
        pieces, (reach_ref, out, e_buf, c_buf, e_sem, c_sem) = refs[:-6], refs[-6:]
        core = lax.axis_index("blk") % CORES
        c_copies, e_copies = [], []
        for d in range(PIECES):
            cut = pl.ds(d * deep, deep)
            src = pieces[d] if len(pieces) > 1 else pieces[0].at[:, cut]
            c_copies.append(pltpu.make_async_copy(src, c_buf.at[:, cut], c_sem.at[d]))
            c_copies[-1].start()
            for s in range(n_sets):
                e_copies.append(
                    pltpu.make_async_copy(
                        sets[s].at[:, cut], e_buf.at[s, :, cut], e_sem.at[s, d]
                    )
                )
                e_copies[-1].start()
        for d in range(PIECES):
            cut = slice(d * deep, (d + 1) * deep)
            c_copies[d].wait()
            for s in range(n_sets):
                e_copies[d * n_sets + s].wait()
                part = product(e_buf[s, :, cut], c_buf[:, cut], 1, 1)
                here = slice(s * rows, (s + 1) * rows)
                if d:
                    part = out[here] + part
                if d == PIECES - 1:
                    at = hop + (1 - 2 * core) * (s % CORES)
                    seen = (reach_ref[here] > at) & (at >= 0)
                    seen = jnp.where(seen, 1.0, 0.0)
                    seen = jnp.concatenate([seen] * (n_centers // LANES), axis=1)
                    part = jnp.exp(sharpness * part) * seen
                out[here] = part

    return pl.pallas_call(
        body,
        out_shape=shape(n_sets * rows, n_centers),
        in_specs=[ANY] * (n_sets + len(center_pieces))
        + [pl.BlockSpec(memory_space=pltpu.VMEM)],
        out_specs=pl.BlockSpec(memory_space=pltpu.VMEM),
        scratch_shapes=[
            pltpu.VMEM((n_sets, rows, features), F32),
            pltpu.VMEM((n_centers, features), F32),
            pltpu.SemaphoreType.DMA((n_sets, PIECES)),
            pltpu.SemaphoreType.DMA((PIECES,)),
        ],
    )(*row_sets, *center_pieces, reach)


def whole(a):
    return pl.BlockSpec(a.shape, lambda i: (0, 0))


def predicted_early(kernels, coeff_chunks, targets, rows):
    n_rows, n_centers = kernels[0].shape
    wide = coeff_chunks[0][0].shape[1]
    n_k, n_t = len(kernels), len(targets)

    def body(*refs):
        ks = refs[:n_k]
        ws = refs[n_k : n_k + n_k * CHUNKS]
        ts = refs[n_k + n_k * CHUNKS : -1]
        out = refs[-1]
        for i in range(CHUNKS):
            out[:, i * wide : (i + 1) * wide] = sum(
                product(ks[j][...], ws[j * CHUNKS + i][...], 1, 0) for j in range(n_k)
            )
        for s in range(n_t):

            @pl.when(pl.program_id(0) == CORES * s)
            def _():
                out[...] -= ts[s][...]

    flat = [w for chunks in coeff_chunks for w in chunks]
    return pl.pallas_call(
        body,
        grid=(n_rows // rows,),
        out_shape=shape(n_rows, wide * CHUNKS),
        in_specs=[pl.BlockSpec((rows, n_centers), lambda i: (i, 0))] * n_k
        + [whole(a) for a in flat + list(targets)],
        out_specs=pl.BlockSpec((rows, wide * CHUNKS), lambda i: (i, 0)),
    )(*kernels, *flat, *targets)


def predicted_last(early, kernel, coeff_chunk, chunk, rows):
    n_rows, n_centers = kernel.shape
    wide = coeff_chunk.shape[1]

    def body(p, k, w, out):
        out[...] = p[...] + product(k[...], w[...], 1, 0)

    return pl.pallas_call(
        body,
        grid=(n_rows // rows,),
        out_shape=shape(n_rows, wide),
        in_specs=[
            pl.BlockSpec((rows, wide), lambda i: (i, chunk)),
            pl.BlockSpec((rows, n_centers), lambda i: (i, 0)),
            whole(coeff_chunk),
        ],
        out_specs=pl.BlockSpec((rows, wide), lambda i: (i, 0)),
    )(early, kernel, coeff_chunk)


def residual_gradient(mine, other, kernel, rows):
    n_rows, n_centers = kernel.shape
    wide = mine.shape[1]

    def body(p, q, k, r_out, g_out):
        r = p[...] + q[...]
        r_out[...] = r
        g = product(k[...], r, 0, 0)

        @pl.when(pl.program_id(0) == 0)
        def _():
            g_out[...] = g

        @pl.when(pl.program_id(0) > 0)
        def _():
            g_out[...] += g

    return pl.pallas_call(
        body,
        grid=(n_rows // rows,),
        out_shape=[shape(n_rows, wide), shape(n_centers, wide)],
        in_specs=[
            pl.BlockSpec((rows, wide), lambda i: (i, 0)),
            pl.BlockSpec((rows, wide), lambda i: (i + 1 - 2 * (i % CORES), 0)),
            pl.BlockSpec((rows, n_centers), lambda i: (i, 0)),
        ],
        out_specs=[
            pl.BlockSpec((rows, wide), lambda i: (i, 0)),
            pl.BlockSpec((n_centers, wide), lambda i: (0, 0)),
        ],
    )(mine, other, kernel)


def gradients(kernels, residual, rows):
    n_rows, n_centers = kernels[0].shape
    wide = residual.shape[1]
    n_k = len(kernels)

    def body(*refs):
        r = refs[n_k][...]
        for k, out in zip(refs[:n_k], refs[n_k + 1 :]):
            g = product(k[...], r, 0, 0)

            @pl.when(pl.program_id(0) == 0)
            def _():
                out[...] = g

            @pl.when(pl.program_id(0) > 0)
            def _():
                out[...] += g

    return pl.pallas_call(
        body,
        grid=(n_rows // rows,),
        out_shape=[shape(n_centers, wide)] * n_k,
        in_specs=[pl.BlockSpec((rows, n_centers), lambda i: (i, 0))] * n_k
        + [pl.BlockSpec((rows, wide), lambda i: (i, 0))],
        out_specs=[pl.BlockSpec((n_centers, wide), lambda i: (0, 0))] * n_k,
    )(*kernels, residual)


def on_device(examples, targets, hop_reach, centers, coeffs, step_gain):
    rows, features = examples.shape
    outputs = targets.shape[1]
    n_rep = lax.axis_size("rep")
    rep = lax.axis_index("rep")
    odd = (lax.axis_index("blk") // CORES) % 2 == 1
    far = 2 * CORES
    sharpness = 0.5 / math.sqrt(features)
    half = -(-outputs // (n_rep * LANES)) * LANES

    row_sets, reaches = [], []
    for s in range(n_rep):
        e = shifted(examples, "rep", s) if s else examples
        r = shifted(hop_reach, "rep", s) if s else hop_reach
        row_sets += [e, swapped(e, 1)]
        reaches.append(r)
    mine = jnp.stack(reaches)
    both = jnp.stack([mine, swapped(mine, 1)], axis=1)
    reach = jnp.broadcast_to(both.reshape(-1)[:, None], (both.size, LANES))

    c0 = split(centers)
    prepared = halves(coeffs, targets, n_rep, half)
    w0, target_sets = prepared[:CHUNKS], prepared[CHUNKS:]
    c2 = [shifted(p, "blk", far) for p in c0]
    w2 = [shifted(p, "blk", far) for p in w0]
    c1, w1 = [], []
    for own, received in zip(c0, c2):
        c1.append(swapped(relay(own, received), CORES))
    for own, received in zip(w0, w2):
        w1.append(swapped(relay(own, received), CORES))
    target_sets = [target_sets[0]] + [
        shifted(target_sets[s], "rep", s) for s in range(1, n_rep)
    ]

    k0 = kernel_block(row_sets, [centers], reach, 0, sharpness)
    k2 = kernel_block(row_sets, c2, reach, 2 * CORES, sharpness)
    k1 = kernel_block(row_sets, c1, reach, CORES, sharpness)
    early = predicted_early([k0, k2], [w0, w2], target_sets, rows)

    step_size = 1.0 / math.sqrt(rows * n_rep * (HOPS + 1))
    factor = (step_size * step_gain)[:, None]
    residuals = [[] for _ in range(n_rep)]
    updated = [[] for _ in range(n_rep)]
    for i in range(CHUNKS):
        mine = predicted_last(early, k1, w1[i], i, rows)
        other = swapped(mine, 1)
        r, g1 = residual_gradient(mine, other, k1, rows)
        across = swapped(g1, CORES)
        g0, g2 = gradients([k0, k2], r, rows)
        onward = g2 + jnp.where(odd, across, 0.0)
        back = shifted(onward, "blk", -far)
        new = w0[i] - factor * (g0 + jnp.where(odd, 0.0, across) + back)
        for s in range(n_rep):
            part = r[CORES * s * rows : (CORES * s + 1) * rows]
            residuals[s].append(shifted(part, "rep", -s) if s else part)
            updated[s].append(shifted(new, "rep", -s) if s else new)

    def assembled(received):
        parts = [jnp.concatenate(p, axis=1) for p in received]
        placed = []
        for q in range(n_rep):
            part = parts[0]
            for s in range(1, n_rep):
                part = jnp.where((rep + s) % n_rep == q, parts[s], part)
            placed.append(part)
        return jnp.concatenate(placed, axis=1)[:, :outputs]

    return (assembled(updated), assembled(residuals))


def solution(mesh):
    in_specs = (
        P(("blk", "rep"), None),
        P(("blk", "rep"), None),
        P(("blk", "rep")),
        P("blk", None),
        P("blk", None),
        P("blk"),
    )
    out_specs = (P("blk", None), P(("blk", "rep"), None))

    return jax.shard_map(
        on_device, mesh=mesh, in_specs=in_specs, out_specs=out_specs, check_vma=False
    )
```
